256 devices in a mesh: sa: 4 (over z_hi), sb: 8 (over x, core), rep: 8 (over z_lo, y).
Axes of the slice: x: 4, y: 4, z: 8 (z_hi: 4, z_lo: 2; z = z_hi * 2 + z_lo), core: 2. Of those that a mesh axis runs over, the one named last changes fastest.
Arguments:
- queries: bfloat16 [8, 64, 64, 12288], P('rep', ('sa', 'sb')), may hold values from -90.93267 to 90.93267
- grad_out: bfloat16 [8, 64, 64, 8192], P('rep', ('sa', 'sb')), may hold values from -6 to 6
- cache_codes: bfloat16 [8, 320, 16, 576], P('rep', ('sa', 'sb')), may hold values from -4.1 to 4.1
- cache_exponents: int32 [8, 320, 16, 4], P('rep', ('sa', 'sb')), may hold values from -1 to 1
- page_table: int32 [8, 64, 5], P('rep'), may hold values from 0 to 319, as said below
- offsets: int32 [8, 64], P('rep'), may hold values from 8 to 16, as said below
- key_up: bfloat16 [64, 512, 128], P(('sa', 'sb')), may hold values from -0.25 to 0.25
- value_up: bfloat16 [64, 512, 128], P(('sa', 'sb')), may hold values from -0.25 to 0.25
Outputs:
- grad_queries: bfloat16 [8, 64, 64, 12288], P('rep', ('sa', 'sb'))
- grad_cache: float32 [8, 320, 16, 576], P('rep', ('sa', 'sb'))
- grad_key_up: float32 [64, 512, 128], P(('sa', 'sb'))
- grad_value_up: float32 [64, 512, 128], P(('sa', 'sb'))
The draws below stay inside these ranges and needn't reach their ends.
Inputs may be any that keep to these rules, and one draw needn't show every extreme that they name: `page_table`: the rows of the sequences of one replica together name each of that replica's 320 pool pages exactly once. Query i of sequence s of replica r stands at key position offsets[r, s] + i.
All inputs are finite; a program needn't handle non-finite values.
Results may differ from the reference program's by a relative error of at most 0.015.
Values may be sent and summed in bfloat16 or wider, within the bound.
No kernel may reach another device: no remote copies, remote signals or barrier semaphores. Data moves between devices by JAX's collectives and lax.ppermute only.
A program may use at most 128 MiB of HBM per device.

```python
import jax
import jax.numpy as jnp
from jax import lax

H = 64
RANK = 512
ROPE = 64
NOPE = 128
VDIM = 128
SCALES = 4
PAGE = 16
SEQ_REP = 64
Q = 64
PREFIX = 16
CTX = 80
PAGES_REP = 320
REPLICAS = 8


def shuffle_pages(single_key):
    return jax.random.permutation(single_key, PAGES_REP)


def layout(key):
    base_key = jax.random.fold_in(key, 7001)
    total_seqs = REPLICAS * SEQ_REP
    page_keys = jax.random.split(jax.random.fold_in(base_key, 1), REPLICAS)
    pages_map = jax.vmap(shuffle_pages)(page_keys).reshape(REPLICAS, SEQ_REP, CTX // PAGE).astype(jnp.int32)
    starts = jax.random.randint(jax.random.fold_in(base_key, 2), (total_seqs,), PREFIX // 2, PREFIX + 1)
    chosen = jax.random.permutation(jax.random.fold_in(base_key, 3), total_seqs)
    starts = starts.at[chosen[0]].set(PREFIX).at[chosen[1]].set(PREFIX // 2)
    return (pages_map, starts.reshape(REPLICAS, SEQ_REP).astype(jnp.int32))


def pool_values(key):
    full_shape = (REPLICAS, PAGES_REP, PAGE, RANK + ROPE)
    inner_key = jax.random.fold_in(key, 7002)
    values = jax.random.truncated_normal(inner_key, -4.0, 4.0, full_shape, jnp.float32)
    return values


def draw_cache_codes(key, part):
    values = pool_values(key)
    return values.astype(jnp.bfloat16)


def draw_queries(key, part):
    total_seqs = REPLICAS * SEQ_REP
    full_shape = (total_seqs, Q, H, NOPE + ROPE)
    inner_key = jax.random.fold_in(key, 7003)
    values = jax.random.truncated_normal(inner_key, -4.0, 4.0, full_shape, jnp.float32)
    return values.reshape(REPLICAS, SEQ_REP, Q, H * (NOPE + ROPE)).astype(jnp.bfloat16)


def draw_page_table(key, part):
    return layout(key)[0]


def draw_offsets(key, part):
    return layout(key)[1]


def set_ends(values, key, least, high):
    place = [jax.random.randint(jax.random.fold_in(key, axis), (), 0, length) for axis, length in enumerate(values.shape)]
    longest = values.shape.index(max(values.shape))
    neighbour = place[:longest] + [(place[longest] + 1) % values.shape[longest]] + place[longest + 1:]
    return values.at[tuple(place)].set(least).at[tuple(neighbour)].set(high)


def level_of(rng, extent, cuts, smallest, largest):
    gain, own = 1.0, jax.random.fold_in(rng, 6)
    for axis_at, shards_of in cuts:
        heights = jnp.exp(jax.random.uniform(jax.random.fold_in(own, axis_at), (shards_of,), jnp.float32, smallest / len(cuts), largest / len(cuts)))
        gain = gain * jnp.repeat(heights, extent[axis_at] // shards_of).reshape([-1 if axis == axis_at else 1 for axis in range(len(extent))])
    return gain


def centred(stream_key, shape, scale, limit, cuts=(), kind=jnp.bfloat16):
    entries = scale * jax.random.normal(stream_key, shape, jnp.float32)
    if cuts:
        entries = entries * level_of(stream_key, shape, cuts, -0.22, 0.18)
    return jnp.clip(entries, -limit, limit).astype(kind)


def setup_inputs(seed: int = 0) -> dict:
    splits = jax.random.split(jax.random.key(seed), 9)
    queries = draw_queries(jax.random.fold_in(splits[8], 71), 0)
    grad_out = centred(splits[1], (REPLICAS, SEQ_REP, Q, H * VDIM), 1.0, 6.0, ((0, 8), (1, 32)))
    cache_codes = draw_cache_codes(jax.random.fold_in(splits[8], 71), 0)
    cache_exponents = set_ends(jax.random.randint(splits[3], (REPLICAS, PAGES_REP, PAGE, SCALES), -1, 2), jax.random.fold_in(splits[3], 1), -1, 1).astype(jnp.int32)
    page_table = draw_page_table(jax.random.fold_in(splits[8], 71), 0)
    offsets = draw_offsets(jax.random.fold_in(splits[8], 71), 0)
    key_up = centred(splits[6], (H, RANK, NOPE), RANK ** -0.5, 0.25, ((0, 32),))
    value_up = centred(splits[7], (H, RANK, VDIM), RANK ** -0.5, 0.25, ((0, 32),))
    return dict(queries=queries, grad_out=grad_out, cache_codes=cache_codes, cache_exponents=cache_exponents, page_table=page_table, offsets=offsets, key_up=key_up, value_up=value_up)


def rounded(value):
    return lax.optimization_barrier(value.astype(jnp.bfloat16)).astype(jnp.float32)


def dequantize(stored, exponents):
    block_size = RANK // exponents.shape[-1]
    factor = jnp.repeat(jnp.exp2(exponents.astype(jnp.float32)), block_size, axis=-1)
    latent = (stored[..., :RANK].astype(jnp.float32) * factor).astype(jnp.bfloat16)
    return jnp.concatenate([latent, stored[..., RANK:]], axis=-1)


def sequence_grads(query_rows, grad_rows, seq_keys, start, key_up, value_up):
    head_count = key_up.shape[0]
    row_count = query_rows.shape[0]
    key_count = seq_keys.shape[0]
    softmax_scale = (NOPE + ROPE) ** -0.5
    split_rows = query_rows.reshape(row_count, head_count, NOPE + ROPE).astype(jnp.float32)
    query_nope = split_rows[:, :, :NOPE]
    query_rope = jnp.transpose(split_rows[:, :, NOPE:], (1, 0, 2))
    up_keys = key_up.astype(jnp.float32)
    up_values = value_up.astype(jnp.float32)
    keys_wide = seq_keys.astype(jnp.float32)
    latent = keys_wide[:, :RANK]
    query_lat = rounded(jnp.einsum("qhd,hrd->hqr", query_nope, up_keys))
    query_full = jnp.concatenate([query_lat, query_rope], axis=-1)
    scores = jnp.einsum("hqc,kc->hqk", query_full, keys_wide) * softmax_scale
    position = start + jnp.arange(row_count, dtype=jnp.int32)
    visible = jnp.arange(key_count, dtype=jnp.int32)[None, :] <= position[:, None]
    scores = jnp.where(visible[None], scores, -jnp.inf)
    row_max = jnp.max(scores, axis=-1, keepdims=True)
    exp_scores = jnp.exp(scores - row_max)
    attention = exp_scores / jnp.sum(exp_scores, axis=-1, keepdims=True)
    attention_low = rounded(attention)
    out_latent = jnp.einsum("hqk,kr->hqr", attention_low, latent)
    grad_split = grad_rows.reshape(row_count, head_count, VDIM).astype(jnp.float32)
    grad_latent = jnp.einsum("qhv,hrv->hqr", grad_split, up_values)
    grad_latent_low = rounded(grad_latent)
    row_delta = jnp.sum(grad_latent * out_latent, axis=-1, keepdims=True)
    grad_attention = jnp.einsum("hqr,kr->hqk", grad_latent_low, latent)
    grad_scores = rounded(attention * (grad_attention - row_delta) * softmax_scale)
    grad_full = jnp.einsum("hqk,kc->hqc", grad_scores, keys_wide)
    grad_qlat = rounded(grad_full[..., :RANK])
    grad_nope = jnp.einsum("hqr,hrd->qhd", grad_qlat, up_keys)
    grad_rope = jnp.transpose(grad_full[..., RANK:], (1, 0, 2))
    grad_query = jnp.concatenate([grad_nope, grad_rope], axis=-1)
    grad_query = grad_query.reshape(row_count, head_count * (NOPE + ROPE)).astype(jnp.bfloat16)
    grad_keys = jnp.einsum("hqk,hqc->kc", grad_scores, query_full)
    grad_values = jnp.einsum("hqk,hqr->kr", attention_low, grad_latent_low)
    grad_keys = grad_keys + jnp.pad(grad_values, ((0, 0), (0, ROPE)))
    grad_key_up = jnp.einsum("hqr,qhd->hrd", grad_qlat, query_nope)
    grad_value_up = jnp.einsum("hqr,qhv->hrv", rounded(out_latent), grad_split)
    return grad_query, grad_keys, grad_key_up, grad_value_up


def reference(queries, grad_out, cache_codes, cache_exponents, page_table, offsets, key_up, value_up):
    key_pool = dequantize(cache_codes, cache_exponents)
    total_seqs = REPLICAS * SEQ_REP
    flat_queries = queries.reshape(total_seqs, Q, H * (NOPE + ROPE))
    flat_grads = grad_out.reshape(total_seqs, Q, H * VDIM)
    flat_table = page_table.reshape(total_seqs, CTX // PAGE)
    flat_offsets = offsets.reshape(total_seqs)

    def seq_step(totals, seq_index):
        replica = seq_index // SEQ_REP
        seq_keys = key_pool[replica][flat_table[seq_index]].reshape(CTX, RANK + ROPE)
        results = sequence_grads(flat_queries[seq_index], flat_grads[seq_index], seq_keys, flat_offsets[seq_index], key_up, value_up)
        return (totals[0] + results[2], totals[1] + results[3]), (results[0], results[1])

    zero_sums = (jnp.zeros(key_up.shape, jnp.float32), jnp.zeros(value_up.shape, jnp.float32))
    weight_sums, outputs = lax.scan(seq_step, zero_sums, jnp.arange(total_seqs, dtype=jnp.int32))
    grad_queries = outputs[0].reshape(REPLICAS, SEQ_REP, Q, H * (NOPE + ROPE))
    key_pages = outputs[1].reshape(REPLICAS, PAGES_REP, PAGE, RANK + ROPE)
    replica_ids = jnp.arange(REPLICAS, dtype=jnp.int32)[:, None]
    grad_cache = jnp.zeros(key_pages.shape, jnp.float32).at[replica_ids, page_table.reshape(REPLICAS, PAGES_REP)].set(key_pages)
    return grad_queries, grad_cache, weight_sums[0], weight_sums[1]
```

```python
import functools

import jax
import jax.numpy as jnp
from jax import lax
from jax.experimental import pallas as pl
from jax.experimental.pallas import tpu as pltpu
from jax.sharding import PartitionSpec as P

RANK = 512
ROPE = 64
NOPE = 128
VDIM = 128
PAGE = 16
QD = NOPE + ROPE
WIDE = 768
GROUP = ("sa", "sb")
BF16 = jnp.bfloat16
F32 = jnp.float32


def dequantize(stored, exponents):
    block_size = RANK // exponents.shape[-1]
    factor = jnp.repeat(jnp.exp2(exponents.astype(F32)), block_size, axis=-1)
    latent = (stored[..., :RANK].astype(F32) * factor).astype(BF16)
    return jnp.concatenate([latent, stored[..., RANK:]], axis=-1)


def dot_nn(a, b):
    return lax.dot_general(a, b, (((1,), (0,)), ((), ())), preferred_element_type=F32)


def dot_nt(a, b):
    return lax.dot_general(a, b, (((1,), (1,)), ((), ())), preferred_element_type=F32)


def dot_tn(a, b):
    return lax.dot_general(a, b, (((0,), (0,)), ((), ())), preferred_element_type=F32)


def split_kernel(*refs, parts, groups):
    n = len(parts)
    srcs, dsts, sem = refs[:n], refs[n:2 * n], refs[2 * n]
    copies = []
    for k, width in enumerate(parts):
        for g in range(groups[0]):
            for b in range(groups[1]):
                p = g * groups[1] + b
                copies.append(pltpu.make_async_copy(
                    srcs[k].at[:, :, p * width:(p + 1) * width], dsts[k].at[b, :, g], sem.at[len(copies)]))
    for c in copies:
        c.start()
    for c in copies:
        c.wait()


def split_columns(arrays, outer, inner):
    seqs, rows = arrays[0].shape[:2]
    parts = tuple(x.shape[2] // (outer * inner) for x in arrays)
    return pl.pallas_call(
        functools.partial(split_kernel, parts=parts, groups=(outer, inner)),
        in_specs=[pl.BlockSpec(memory_space=pl.ANY)] * len(arrays),
        out_specs=[pl.BlockSpec(memory_space=pl.ANY)] * len(arrays),
        out_shape=[jax.ShapeDtypeStruct((inner, seqs, outer, rows, w), x.dtype) for w, x in zip(parts, arrays)],
        scratch_shapes=[pltpu.SemaphoreType.DMA((len(arrays) * outer * inner,))],
        name="split",
    )(*arrays)


def join_kernel(src, dst, sem, *, width, groups):
    copies = []
    for g in range(groups[0]):
        for b in range(groups[1]):
            p = g * groups[1] + b
            copies.append(pltpu.make_async_copy(
                src.at[b, :, g], dst.at[:, :, p * width:(p + 1) * width], sem.at[len(copies)]))
    for c in copies:
        c.start()
    for c in copies:
        c.wait()


def join_columns(x):
    inner, seqs, outer, rows, width = x.shape
    return pl.pallas_call(
        functools.partial(join_kernel, width=width, groups=(outer, inner)),
        in_specs=[pl.BlockSpec(memory_space=pl.ANY)],
        out_specs=pl.BlockSpec(memory_space=pl.ANY),
        out_shape=jax.ShapeDtypeStruct((seqs, rows, outer * inner * width), x.dtype),
        scratch_shapes=[pltpu.SemaphoreType.DMA((outer * inner,))],
        name="join",
    )(x)


def grads_kernel(offs_ref, q_ref, go_ref, w_ref, keys_ref, dq_ref, dkeys_ref, dw_ref, stash, lat_t, *, rows, ctx):
    step = pl.program_id(0)
    pairs = w_ref.shape[0]
    scale = QD ** -0.5
    both = 2 * ctx
    wide = 2 * (NOPE + VDIM)
    base = pl.multiple_of(step * both, both)
    here = pl.ds(base, both)

    lane = lax.broadcasted_iota(jnp.int32, (ctx, 2 * rows), 1)
    first = lane < rows
    limit = jnp.where(first, lane + offs_ref[2 * step], lane - rows + offs_ref[2 * step + 1])
    visible = lax.broadcasted_iota(jnp.int32, (ctx, 2 * rows), 0) <= limit
    lat = keys_ref[here, :RANK]
    rope = keys_ref[here, RANK:]
    zero = jnp.zeros((ctx, 2 * rows), F32)

    def pack(x):
        return jnp.where(first, x[:ctx], x[ctx:])

    def spread(x):
        return jnp.concatenate([jnp.where(first, x, zero), jnp.where(first, zero, x)], axis=0).astype(BF16)

    d_lat = None
    d_rope = None
    for g in range(pairs):
        kv = dot_nn(lat, w_ref[g]).astype(BF16)
        for h in range(2):
            q = q_ref[:, g, :, h * QD:(h + 1) * QD].reshape(2 * rows, QD)
            go = go_ref[:, g, :, h * VDIM:(h + 1) * VDIM].reshape(2 * rows, VDIM)
            c = h * (NOPE + VDIM)
            k = jnp.concatenate([kv[:, c:c + NOPE], rope], axis=1)
            v = kv[:, c + NOPE:c + NOPE + VDIM]
            s = jnp.where(visible, pack(dot_nt(k, q)) * scale, -jnp.inf)
            e = jnp.exp(s - jnp.max(s, axis=0, keepdims=True))
            a = e / jnp.sum(e, axis=0, keepdims=True)
            a_low = a.astype(BF16).astype(F32)
            da = pack(dot_nt(v, go))
            delta = jnp.sum(a_low * da, axis=0, keepdims=True)
            ds = a * (da - delta) * scale
            a_bd = spread(a_low)
            ds_bd = spread(ds)
            dv = dot_nn(a_bd, go).astype(BF16)
            dk = dot_nn(ds_bd, q)
            dq = dot_tn(ds_bd, k)
            dq_ref[:, g, :, h * QD:(h + 1) * QD] = dq.astype(BF16).reshape(2, rows, QD)
            stash[here, g * wide + c:g * wide + c + NOPE] = dk[:, :NOPE].astype(BF16)
            stash[here, g * wide + c + NOPE:g * wide + c + NOPE + VDIM] = dv
            d_rope = dk[:, NOPE:] if d_rope is None else d_rope + dk[:, NOPE:]
        part = dot_nt(stash[here, g * wide:(g + 1) * wide], w_ref[g])
        d_lat = part if d_lat is None else d_lat + part
    dkeys_ref[:, :RANK] = d_lat.astype(BF16)
    dkeys_ref[:, RANK:] = d_rope.astype(BF16)

    @pl.when(step == pl.num_programs(0) - 1)
    def _():
        lat_t[...] = keys_ref[:, :RANK].T
        slots = dw_ref.shape[0]
        for g in range(pairs):
            dw = dot_nn(lat_t[...], stash[:, g * wide:(g + 1) * wide]).astype(BF16)
            dw_ref[:, g] = dw.reshape(slots, RANK // slots, wide)


def sequence_grads(queries, grad_out, keys, offs, weights, slots):
    seqs, pairs, rows, qw = queries.shape
    gw = grad_out.shape[3]
    wide = weights.shape[2]
    total = keys.shape[0]
    ctx = total // seqs
    grid_spec = pltpu.PrefetchScalarGridSpec(
        num_scalar_prefetch=1,
        grid=(seqs // 2,),
        in_specs=[
            pl.BlockSpec((2, pairs, rows, qw), lambda i, *_: (i, 0, 0, 0)),
            pl.BlockSpec((2, pairs, rows, gw), lambda i, *_: (i, 0, 0, 0)),
            pl.BlockSpec((pairs, RANK, wide), lambda i, *_: (0, 0, 0)),
            pl.BlockSpec((total, RANK + ROPE), lambda i, *_: (0, 0)),
        ],
        out_specs=[
            pl.BlockSpec((2, pairs, rows, qw), lambda i, *_: (i, 0, 0, 0)),
            pl.BlockSpec((2 * ctx, RANK + ROPE), lambda i, *_: (i, 0)),
            pl.BlockSpec((slots, pairs, RANK // slots, wide), lambda i, *_: (0, 0, 0, 0)),
        ],
        scratch_shapes=[
            pltpu.VMEM((total, pairs * wide), BF16),
            pltpu.VMEM((RANK, total), BF16),
        ],
    )
    return pl.pallas_call(
        functools.partial(grads_kernel, rows=rows, ctx=ctx),
        grid_spec=grid_spec,
        out_shape=[
            jax.ShapeDtypeStruct(queries.shape, BF16),
            jax.ShapeDtypeStruct((total, RANK + ROPE), BF16),
            jax.ShapeDtypeStruct((slots, pairs, RANK // slots, wide), BF16),
        ],
        name="grads",
    )(offs, queries, grad_out, weights, keys)


def swap(x, axes):
    return lax.all_to_all(x, axes, split_axis=0, concat_axis=0, tiled=True)


def to_pieces(pages, devices):
    count = pages.shape[0]
    wide = jnp.pad(pages.reshape(count, PAGE, RANK + ROPE), ((0, 0), (0, 0), (0, WIDE - RANK - ROPE)))
    return wide.reshape(count, devices, -1).transpose(1, 0, 2)


def from_pieces(pieces):
    devices, count, width = pieces.shape
    return pieces.transpose(1, 0, 2).reshape(count, PAGE, WIDE)[:, :, :RANK + ROPE]


def route(pages, choose, devices):
    pieces = swap(to_pieces(pages, devices), GROUP)
    rows = dot_nn(choose, pieces.reshape(-1, pieces.shape[2])).astype(BF16)
    return from_pieces(swap(rows.reshape(pieces.shape), GROUP))


def local(queries, grad_out, cache_codes, cache_exponents, page_table, offsets, key_up, value_up):
    seqs = queries.shape[1]
    n_a, n_b, n_rep = lax.axis_size("sa"), lax.axis_size("sb"), lax.axis_size("rep")
    devices = n_a * n_b
    a_index = lax.axis_index("sa")
    flat = page_table[0].reshape(-1)
    ids = jnp.arange(flat.shape[0], dtype=jnp.int32)
    pick = (flat[:, None] == ids[None]).astype(BF16)
    put = (ids[:, None] == flat[None]).astype(BF16)
    offs = lax.dynamic_slice_in_dim(offsets[0], a_index * seqs * n_b, seqs * n_b, 0)

    own_keys = route(dequantize(cache_codes, cache_exponents)[0], pick, devices).reshape(-1, RANK + ROPE)
    keys = swap(jnp.broadcast_to(own_keys[None], (n_b,) + own_keys.shape), "sb").reshape(-1, RANK + ROPE)

    w = jnp.concatenate([key_up[0], value_up[0], key_up[1], value_up[1]], axis=1)
    weights = swap(jnp.broadcast_to(w[None], (n_a,) + w.shape), "sa")

    q_out, g_out = split_columns((queries[0], grad_out[0]), n_a, n_b)
    q_in = swap(q_out, "sb")
    g_in = swap(g_out, "sb")
    q_in = q_in.reshape((-1,) + q_in.shape[2:])
    g_in = g_in.reshape((-1,) + g_in.shape[2:])

    dq, dkeys, dw = sequence_grads(q_in, g_in, keys, offs, weights, n_rep)

    dq = swap(dq.reshape(q_out.shape), "sb")
    grad_queries = join_columns(dq)[None]

    key_parts = swap(dkeys.reshape(n_b, -1, RANK + ROPE), "sb")
    own = jnp.sum(key_parts.astype(F32), axis=0).astype(BF16)
    grad_cache = route(own.reshape(-1, PAGE, RANK + ROPE), put, devices).astype(F32)[None]

    def add(x):
        return jnp.sum(x.astype(F32), axis=0).astype(BF16)

    dw = add(swap(add(swap(dw, "rep")), "sa"))
    dw = swap(jnp.broadcast_to(dw[None], (n_rep,) + dw.shape), "rep").reshape(RANK, -1).astype(F32)
    dw = jnp.transpose(dw.reshape(RANK, 2, 2, NOPE), (2, 1, 0, 3))
    return grad_queries, grad_cache, dw[0], dw[1]


def solution(mesh):
    in_specs = (
        P("rep", ("sa", "sb"), None, None),
        P("rep", ("sa", "sb"), None, None),
        P("rep", ("sa", "sb"), None, None),
        P("rep", ("sa", "sb"), None, None),
        P("rep", None, None),
        P("rep", None),
        P(("sa", "sb"), None, None),
        P(("sa", "sb"), None, None),
    )
    out_specs = (
        P("rep", ("sa", "sb"), None, None),
        P("rep", ("sa", "sb"), None, None),
        P(("sa", "sb"), None, None),
        P(("sa", "sb"), None, None),
    )
    return jax.shard_map(local, mesh=mesh, in_specs=in_specs, out_specs=out_specs, check_vma=False)
```

```python
import functools

import jax
import jax.numpy as jnp
from jax import lax
from jax.experimental import pallas as pl
from jax.experimental.pallas import tpu as pltpu
from jax.sharding import PartitionSpec as P

RANK = 512
ROPE = 64
NOPE = 128
VDIM = 128
PAGE = 16
QD = NOPE + ROPE
WIDE = 768
GROUP = ("sa", "sb")
BF16 = jnp.bfloat16
F32 = jnp.float32


def dequantize(stored, exponents):
    block_size = RANK // exponents.shape[-1]
    factor = jnp.repeat(jnp.exp2(exponents.astype(F32)), block_size, axis=-1)
    latent = (stored[..., :RANK].astype(F32) * factor).astype(BF16)
    return jnp.concatenate([latent, stored[..., RANK:]], axis=-1)


def dot_nn(a, b):
    return lax.dot_general(a, b, (((1,), (0,)), ((), ())), preferred_element_type=F32)


def dot_nt(a, b):
    return lax.dot_general(a, b, (((1,), (1,)), ((), ())), preferred_element_type=F32)


def dot_tn(a, b):
    return lax.dot_general(a, b, (((0,), (0,)), ((), ())), preferred_element_type=F32)


def split_kernel(*refs):
    n = len(refs) // 2
    for src, dst in zip(refs[:n], refs[n:]):
        width = dst.shape[4]
        for b in range(dst.shape[0]):
            dst[b, :, 0] = src[:, :, b * width:(b + 1) * width]


def split_columns(arrays, outer, inner):
    seqs, rows = arrays[0].shape[:2]
    widths = [x.shape[2] // (outer * inner) for x in arrays]
    return pl.pallas_call(
        split_kernel,
        grid=(outer,),
        in_specs=[pl.BlockSpec((seqs, rows, inner * w), lambda g: (0, 0, g)) for w in widths],
        out_specs=[pl.BlockSpec((inner, seqs, 1, rows, w), lambda g: (0, 0, g, 0, 0)) for w in widths],
        out_shape=[jax.ShapeDtypeStruct((inner, seqs, outer, rows, w), x.dtype) for w, x in zip(widths, arrays)],
        name="split",
    )(*arrays)


def join_kernel(src, dst):
    width = src.shape[4]
    for b in range(src.shape[0]):
        dst[:, :, b * width:(b + 1) * width] = src[b, :, 0]


def join_columns(x):
    inner, seqs, outer, rows, width = x.shape
    return pl.pallas_call(
        join_kernel,
        grid=(outer,),
        in_specs=[pl.BlockSpec((inner, seqs, 1, rows, width), lambda g: (0, 0, g, 0, 0))],
        out_specs=pl.BlockSpec((seqs, rows, inner * width), lambda g: (0, 0, g)),
        out_shape=jax.ShapeDtypeStruct((seqs, rows, outer * inner * width), x.dtype),
        name="join",
    )(x)


def grads_kernel(offs_ref, order_ref, q_ref, go_ref, *refs, pairs, rows, ctx):
    w_refs, (keys_ref, dq_ref, dkeys_ref, dw_ref, stash, lat_t) = refs[:pairs], refs[pairs:]
    step = pl.program_id(0)
    scale = QD ** -0.5
    both = 2 * ctx
    wide = 2 * (NOPE + VDIM)
    base = pl.multiple_of(step * both, both)
    here = pl.ds(base, both)

    lane = lax.broadcasted_iota(jnp.int32, (ctx, 2 * rows), 1)
    first = lane < rows
    limit = jnp.where(first, lane + offs_ref[2 * step], lane - rows + offs_ref[2 * step + 1])
    visible = lax.broadcasted_iota(jnp.int32, (ctx, 2 * rows), 0) <= limit
    lat = keys_ref[here, :RANK]
    rope = keys_ref[here, RANK:]
    zero = jnp.zeros((ctx, 2 * rows), F32)

    def pack(x):
        return jnp.where(first, x[:ctx], x[ctx:])

    def spread(x):
        return jnp.concatenate([jnp.where(first, x, zero), jnp.where(first, zero, x)], axis=0).astype(BF16)

    d_lat = None
    d_rope = None
    for g in range(pairs):
        w = w_refs[g][...]
        to = order_ref[g]
        kv = dot_nn(lat, w).astype(BF16)
        for h in range(2):
            q = q_ref[:, to, :, h * QD:(h + 1) * QD].reshape(2 * rows, QD)
            go = go_ref[:, to, :, h * VDIM:(h + 1) * VDIM].reshape(2 * rows, VDIM)
            c = h * (NOPE + VDIM)
            k = jnp.concatenate([kv[:, c:c + NOPE], rope], axis=1)
            v = kv[:, c + NOPE:c + NOPE + VDIM]
            s = jnp.where(visible, pack(dot_nt(k, q)) * scale, -jnp.inf)
            e = jnp.exp(s - jnp.max(s, axis=0, keepdims=True))
            a = e / jnp.sum(e, axis=0, keepdims=True)
            a_low = a.astype(BF16).astype(F32)
            da = pack(dot_nt(v, go))
            delta = jnp.sum(a_low * da, axis=0, keepdims=True)
            ds = a * (da - delta) * scale
            a_bd = spread(a_low)
            ds_bd = spread(ds)
            dv = dot_nn(a_bd, go).astype(BF16)
            dk = dot_nn(ds_bd, q)
            dq = dot_tn(ds_bd, k)
            dq_ref[:, to, :, h * QD:(h + 1) * QD] = dq.astype(BF16).reshape(2, rows, QD)
            stash[here, g * wide + c:g * wide + c + NOPE] = dk[:, :NOPE].astype(BF16)
            stash[here, g * wide + c + NOPE:g * wide + c + NOPE + VDIM] = dv
            d_rope = dk[:, NOPE:] if d_rope is None else d_rope + dk[:, NOPE:]
        part = dot_nt(stash[here, g * wide:(g + 1) * wide], w)
        d_lat = part if d_lat is None else d_lat + part
    dkeys_ref[:, :RANK] = d_lat.astype(BF16)
    dkeys_ref[:, RANK:] = d_rope.astype(BF16)

    @pl.when(step == pl.num_programs(0) - 1)
    def _():
        lat_t[...] = keys_ref[:, :RANK].T
        slots = dw_ref.shape[0]
        for g in range(pairs):
            dw = dot_nn(lat_t[...], stash[:, g * wide:(g + 1) * wide]).astype(BF16)
            dw_ref[:, order_ref[g]] = dw.reshape(slots, RANK // slots, wide)


def sequence_grads(queries, grad_out, keys, offs, order, weights, slots):
    seqs, pairs, rows, qw = queries.shape
    gw = grad_out.shape[3]
    wide = weights[0].shape[1]
    total = keys.shape[0]
    ctx = total // seqs
    grid_spec = pltpu.PrefetchScalarGridSpec(
        num_scalar_prefetch=2,
        grid=(seqs // 2,),
        in_specs=[
            pl.BlockSpec((2, pairs, rows, qw), lambda i, *_: (i, 0, 0, 0)),
            pl.BlockSpec((2, pairs, rows, gw), lambda i, *_: (i, 0, 0, 0)),
            *[pl.BlockSpec((RANK, wide), lambda i, *_: (0, 0))] * pairs,
            pl.BlockSpec((total, RANK + ROPE), lambda i, *_: (0, 0)),
        ],
        out_specs=[
            pl.BlockSpec((2, pairs, rows, qw), lambda i, *_: (i, 0, 0, 0)),
            pl.BlockSpec((2 * ctx, RANK + ROPE), lambda i, *_: (i, 0)),
            pl.BlockSpec((slots, pairs, RANK // slots, wide), lambda i, *_: (0, 0, 0, 0)),
        ],
        scratch_shapes=[
            pltpu.VMEM((total, pairs * wide), BF16),
            pltpu.VMEM((RANK, total), BF16),
        ],
    )
    return pl.pallas_call(
        functools.partial(grads_kernel, pairs=pairs, rows=rows, ctx=ctx),
        grid_spec=grid_spec,
        out_shape=[
            jax.ShapeDtypeStruct(queries.shape, BF16),
            jax.ShapeDtypeStruct((total, RANK + ROPE), BF16),
            jax.ShapeDtypeStruct((slots, pairs, RANK // slots, wide), BF16),
        ],
        name="grads",
    )(offs, order, queries, grad_out, *weights, keys)


def swap(x, axes):
    return lax.all_to_all(x, axes, split_axis=0, concat_axis=0, tiled=True)


def to_pieces(pages, devices):
    count = pages.shape[0]
    wide = jnp.pad(pages.reshape(count, PAGE, RANK + ROPE), ((0, 0), (0, 0), (0, WIDE - RANK - ROPE)))
    return wide.reshape(count, devices, -1).transpose(1, 0, 2)


def from_pieces(pieces):
    devices, count, width = pieces.shape
    return pieces.transpose(1, 0, 2).reshape(count, PAGE, WIDE)[:, :, :RANK + ROPE]


def route(pages, choose, devices):
    pieces = swap(to_pieces(pages, devices), GROUP)
    rows = dot_nn(choose, pieces.reshape(-1, pieces.shape[2])).astype(BF16)
    return from_pieces(swap(rows.reshape(pieces.shape), GROUP))


def local(queries, grad_out, cache_codes, cache_exponents, page_table, offsets, key_up, value_up):
    seqs = queries.shape[1]
    n_a, n_b, n_rep = lax.axis_size("sa"), lax.axis_size("sb"), lax.axis_size("rep")
    devices = n_a * n_b
    a_index = lax.axis_index("sa")
    flat = page_table[0].reshape(-1)
    ids = jnp.arange(flat.shape[0], dtype=jnp.int32)
    pick = (flat[:, None] == ids[None]).astype(BF16)
    put = (ids[:, None] == flat[None]).astype(BF16)
    offs = lax.dynamic_slice_in_dim(offsets[0], a_index * seqs * n_b, seqs * n_b, 0)

    own_keys = route(dequantize(cache_codes, cache_exponents)[0], pick, devices).reshape(-1, RANK + ROPE)
    keys = swap(jnp.broadcast_to(own_keys[None], (n_b,) + own_keys.shape), "sb").reshape(-1, RANK + ROPE)

    w = jnp.concatenate([key_up[0], value_up[0], key_up[1], value_up[1]], axis=1)
    weights = [w] + [lax.ppermute(w, "sa", [(i, (i + k) % n_a) for i in range(n_a)]) for k in range(1, n_a)]
    order = (a_index - jnp.arange(n_a, dtype=jnp.int32)) % n_a

    q_out, g_out = split_columns((queries[0], grad_out[0]), n_a, n_b)
    q_in = swap(q_out, "sb")
    g_in = swap(g_out, "sb")
    q_in = q_in.reshape((-1,) + q_in.shape[2:])
    g_in = g_in.reshape((-1,) + g_in.shape[2:])

    dq, dkeys, dw = sequence_grads(q_in, g_in, keys, offs, order, weights, n_rep)

    dq = swap(dq.reshape(q_out.shape), "sb")
    grad_queries = join_columns(dq)[None]

    key_parts = swap(dkeys.reshape(n_b, -1, RANK + ROPE), "sb")
    own = jnp.sum(key_parts.astype(F32), axis=0).astype(BF16)
    grad_cache = route(own.reshape(-1, PAGE, RANK + ROPE), put, devices).astype(F32)[None]

    def add(x):
        return jnp.sum(x.astype(F32), axis=0).astype(BF16)

    dw = add(swap(add(swap(dw, "rep")), "sa"))
    dw = swap(jnp.broadcast_to(dw[None], (n_rep,) + dw.shape), "rep").reshape(RANK, -1).astype(F32)
    dw = jnp.transpose(dw.reshape(RANK, 2, 2, NOPE), (2, 1, 0, 3))
    return grad_queries, grad_cache, dw[0], dw[1]


def solution(mesh):
    in_specs = (
        P("rep", ("sa", "sb"), None, None),
        P("rep", ("sa", "sb"), None, None),
        P("rep", ("sa", "sb"), None, None),
        P("rep", ("sa", "sb"), None, None),
        P("rep", None, None),
        P("rep", None),
        P(("sa", "sb"), None, None),
        P(("sa", "sb"), None, None),
    )
    out_specs = (
        P("rep", ("sa", "sb"), None, None),
        P("rep", ("sa", "sb"), None, None),
        P(("sa", "sb"), None, None),
        P(("sa", "sb"), None, None),
    )
    return jax.shard_map(local, mesh=mesh, in_specs=in_specs, out_specs=out_specs, check_vma=False)
```
